128 devices in a mesh: row: 8 (over x_lo, z), col: 16 (over x_hi, y, core).
Axes of the slice: x: 4 (x_hi: 2, x_lo: 2; x = x_hi * 2 + x_lo), y: 4, z: 4, core: 2. Of those that a mesh axis runs over, the one named last changes fastest.
Arguments:
- amplitudes: bfloat16 [16384, 2048], P(('row', 'col')), may hold values from -6 to 6
- integrals: bfloat16 [2048, 49152], P('row', 'col'), may hold values from -0.125 to 0.125
Outputs:
- ladder: bfloat16 [16384, 49152], P(('row', 'col'))
The draws below stay inside these ranges and needn't reach their ends.
All inputs are finite; a program needn't handle non-finite values.
Results may differ from the reference program's by a relative error of at most 0.001.
Values may be sent and summed in bfloat16 or wider, within the bound.
A program may use at most 128 MiB of HBM per device.

```python
import jax
import jax.numpy as jnp
from jax import lax

IJ = 16384
CD = 2048
AB = 49152


def steps_of(key, extent, shards, least, high):
    def one(dim, blocks):
        steps = jax.random.uniform(jax.random.fold_in(jax.random.fold_in(key, 6), dim), (blocks,), jnp.float32, least / len(shards), high / len(shards))
        return jnp.repeat(jnp.exp(steps), extent[dim] // blocks).reshape((-1,) + (1,) * (len(extent) - dim - 1))

    gain = one(*shards[0])
    for cut in shards[1:]:
        gain = gain * one(*cut)
    return gain


def bell_draw(own_key, extent, scale, bound, cuts=(), kind=jnp.bfloat16):
    loudness = steps_of(own_key, extent, cuts, -0.22, 0.18) if cuts else 1.0
    entries = jax.random.normal(own_key, extent, jnp.float32) * scale * loudness
    return jnp.minimum(jnp.maximum(entries, -bound), bound).astype(kind)


def setup_inputs(seed: int = 0) -> dict:
    key_of = jax.random.split(jax.random.key(seed), 3)
    amplitudes = bell_draw(key_of[0], (IJ, CD), 1.0, 6.0, ((0, 128),))
    integrals = bell_draw(key_of[1], (CD, AB), CD ** -0.5, 0.125, ((0, 8), (1, 16)))
    return dict(amplitudes=amplitudes, integrals=integrals)


def reference(amplitudes, integrals):
    blocks = amplitudes.reshape(16, IJ // 16, CD)
    wide = integrals.astype(jnp.float32)

    def one_block(rows):
        return jnp.dot(rows.astype(jnp.float32), wide, preferred_element_type=jnp.float32).astype(jnp.bfloat16)

    return lax.map(one_block, blocks).reshape(IJ, AB)
```

```python
import functools

import jax
import jax.numpy as jnp
from jax import lax
from jax.experimental import pallas as pl
from jax.experimental.pallas import tpu as pltpu
from jax.sharding import PartitionSpec as P

MESH = pl.DeviceIdType.MESH
W = 128


def kernel(steps, amps, ints, out, a_all, b_all, o_all, a_near, a_far, a_core, a_send, b_one, b_two, b_three, b_send, o_recv, o_send):
    row, col = lax.axis_index("row"), lax.axis_index("col")
    hi, lo, y, z, core = col // 8, row // 4, (col // 2) % 4, row % 4, col % 2
    x = hi * 2 + lo

    def at(x, y, z, core):
        return ((x % 2) * 4 + z, (x // 2) * 8 + y * 2 + core)

    def turn(v, by):
        return (v + by) % 4

    def send(src, dst, send_sem, recv_sem, device):
        return pltpu.make_async_remote_copy(
            src_ref=src, dst_ref=dst, send_sem=send_sem, recv_sem=recv_sem, device_id=device, device_id_type=MESH
        )

    def await_bytes(ref, sem):
        pltpu.make_async_copy(ref, ref, sem).wait()

    barrier = pltpu.get_barrier_semaphore()
    ring = [1, 3, 2]
    partners = [at(turn(x, d), y, z, core) for d in ring] + [at(x, y, turn(z, d), core) for d in ring]
    partners += [at(x, turn(y, d), z, core) for d in ring] + [at(x, turn(y, d), z, 1 - core) for d in [0] + ring]
    for device in partners:
        pl.semaphore_signal(barrier, inc=1, device_id=device, device_id_type=MESH)
    pl.semaphore_wait(barrier, len(partners))

    def half(i):
        return pl.ds(pl.multiple_of(i * W, W), W)

    def one(j):
        cols = half(j)
        for d in ring:
            send(ints.at[0, :, cols], b_all.at[j, lo, z, 0, :, half(hi)], b_send.at[j], b_one.at[j], at(turn(x, d), y, z, core)).start()
            send(ints.at[1, :, cols], b_all.at[j, lo, z, 1, :, half(hi)], b_send.at[j], b_one.at[j], at(x, y, turn(z, d), core)).start()
        pltpu.make_async_copy(ints.at[:, :, cols], b_all.at[j, lo, z, :, :, half(hi)], b_one.at[j]).start()

    def two(j):
        await_bytes(b_all.at[j, 0, :, 0], b_one.at[j])
        for d in (1, 3):
            block = b_all.at[j, :, z, 0]
            send(block, block, b_send.at[j], b_two.at[j], at(x, y, turn(z, d), core)).start()
            block = b_all.at[j, lo, :, 1, :, half(hi)]
            send(block, block, b_send.at[j], b_two.at[j], at(turn(x, d), y, z, core)).start()

    def three(j):
        await_bytes(b_all.at[j, :, :, 0], b_two.at[j])
        for i, d in enumerate((1, 3)):
            block = b_all.at[j, i, turn(z, 4 - d), 0]
            send(block, block, b_send.at[j], b_three.at[j], at(x, y, turn(z, d), core)).start()
            source = turn(x, 4 - d)
            block = b_all.at[j, source % 2, pl.ds(2 * i, 2), 1, :, half(source // 2)]
            send(block, block, b_send.at[j], b_three.at[j], at(turn(x, d), y, z, core)).start()

    def deliver(j, y_to):
        for k in range(2):
            for h in range(2):
                src = o_all.at[j, y_to, pl.ds(k * 128, 128), pl.ds(h * W, W)]
                dst = out.at[:, pl.ds(pl.multiple_of((h * 8 + y * 2 + core) * (steps * W) + j * W, W), W)]
                own = jnp.logical_and(y_to == y, core == k)

                @pl.when(own)
                def _():
                    pltpu.make_async_copy(src, dst, o_recv.at[j]).start()

                @pl.when(jnp.logical_not(own))
                def _():
                    send(src, dst, o_send.at[j], o_recv.at[j], at(x, y_to, z, k)).start()

    def compute(j):
        await_bytes(b_all.at[j, 0, :, 0], b_three.at[j])

        def tile(m, _):
            y_to = turn(y, m + 2)
            block = jnp.dot(
                a_all[pl.ds(2 * y_to, 2)].reshape(256, 2048), b_all[j].reshape(16 * 128, 2 * W), preferred_element_type=jnp.float32
            )
            o_all[j, y_to] = block.astype(jnp.bfloat16)
            deliver(j, y_to)
            return 0

        lax.fori_loop(0, 4, tile, 0)

    mine = a_all.at[2 * y + core]

    def amplitudes_start():
        pltpu.make_async_copy(amps, mine, a_core).start()
        send(amps, mine, a_send, a_near, at(x, turn(y, 1), z, core)).start()
        send(amps, mine, a_send, a_near, at(x, turn(y, 3), z, core)).start()
        send(amps, mine, a_send, a_far, at(x, turn(y, 2), z, core)).start()
        send(amps, mine, a_send, a_core, at(x, y, z, 1 - core)).start()

    def to_core(y_of):
        block = a_all.at[2 * y_of + core]
        send(block, block, a_send, a_core, at(x, y, z, 1 - core)).start()

    def step(t, _):
        @pl.when(jnp.logical_and(t >= 2, t < steps + 2))
        def _():
            three(t - 2)

        @pl.when(jnp.logical_and(t >= 1, t < steps + 1))
        def _():
            two(t - 1)

        @pl.when(t < steps)
        def _():
            one(t)

        @pl.when(t == 0)
        def _():
            amplitudes_start()

        @pl.when(t == 2)
        def _():
            await_bytes(a_all.at[pl.ds(0, 2)], a_near)
            to_core(turn(y, 1))
            to_core(turn(y, 3))

        @pl.when(t == 3)
        def _():
            await_bytes(a_all.at[0], a_far)
            to_core(turn(y, 2))
            await_bytes(a_all.at[pl.ds(0, 5)], a_core)

        @pl.when(t >= 3)
        def _():
            compute(t - 3)

        return 0

    lax.fori_loop(0, steps + 3, step, 0)

    await_bytes(a_all.at[pl.ds(0, 7)], a_send)

    def drain(j, _):
        await_bytes(out.at[:, pl.ds(0, 30 * W)], b_send.at[j])
        await_bytes(out.at[pl.ds(0, 112), pl.ds(0, 16 * W)], o_send.at[j])
        await_bytes(out.at[:, pl.ds(0, 16 * W)], o_recv.at[j])
        return 0

    lax.fori_loop(0, steps, drain, 0)


def body(amplitudes, integrals):
    depth, width = integrals.shape
    steps = width // W
    sem = pltpu.SemaphoreType.DMA
    return pl.pallas_call(
        functools.partial(kernel, steps),
        out_shape=jax.ShapeDtypeStruct((128, 16 * width), jnp.bfloat16),
        in_specs=[pl.BlockSpec(memory_space=pl.ANY)] * 2,
        out_specs=pl.BlockSpec(memory_space=pl.ANY),
        scratch_shapes=[
            pltpu.VMEM((8, 128, 2048), jnp.bfloat16),
            pltpu.VMEM((steps, 2, 4, 2, 128, 2 * W), jnp.bfloat16),
            pltpu.VMEM((steps, 4, 256, 2 * W), jnp.bfloat16),
            sem, sem, sem, sem,
            sem((steps,)), sem((steps,)), sem((steps,)), sem((steps,)), sem((steps,)), sem((steps,)),
        ],
        compiler_params=pltpu.CompilerParams(
            collective_id=0, has_side_effects=True, vmem_limit_bytes=67_000_000
        ),
    )(amplitudes, integrals.reshape(2, depth // 2, width))


def solution(mesh):
    placed = (P(("row", "col"), None), P("row", "col"))
    return jax.shard_map(
        body, mesh=mesh, in_specs=placed, out_specs=P(("row", "col"), None), check_vma=False
    )
```

```python
import functools

import jax
import jax.numpy as jnp
from jax import lax
from jax.experimental import pallas as pl
from jax.experimental.pallas import tpu as pltpu
from jax.sharding import PartitionSpec as P

MESH = pl.DeviceIdType.MESH
W = 256
PARTS = 8


def kernel(steps, amps, ints, out, a_all, b_all, o_all, a_near, a_far, a_core, a_send, b_one, b_two, b_three, b_send, o_recv, o_send):
    row, col = lax.axis_index("row"), lax.axis_index("col")
    hi, lo, y, z, core = col // 8, row // 4, (col // 2) % 4, row % 4, col % 2
    x = hi * 2 + lo

    def at(x, y, z, core):
        return ((x % 2) * 4 + z, (x // 2) * 8 + y * 2 + core)

    def turn(v, by):
        return (v + by) % 4

    def send(src, dst, send_sem, recv_sem, device):
        return pltpu.make_async_remote_copy(
            src_ref=src, dst_ref=dst, send_sem=send_sem, recv_sem=recv_sem, device_id=device, device_id_type=MESH
        )

    def await_bytes(ref, sem):
        pltpu.make_async_copy(ref, ref, sem).wait()

    barrier = pltpu.get_barrier_semaphore()
    ring = [1, 3, 2]
    partners = [at(turn(x, d), y, z, core) for d in ring] + [at(x, y, turn(z, d), core) for d in ring]
    partners += [at(x, turn(y, d), z, core) for d in ring] + [at(x, turn(y, d), z, 1 - core) for d in [0] + ring]
    for device in partners:
        pl.semaphore_signal(barrier, inc=1, device_id=device, device_id_type=MESH)
    pl.semaphore_wait(barrier, len(partners))

    def half(i):
        return pl.ds(pl.multiple_of(i * W, W), W)

    def one(j):
        cols = half(j)
        for d in ring:
            send(ints.at[0, :, cols], b_all.at[j, lo, z, 0, :, half(hi)], b_send.at[j], b_one.at[j], at(turn(x, d), y, z, core)).start()
            send(ints.at[1, :, cols], b_all.at[j, lo, z, 1, :, half(hi)], b_send.at[j], b_one.at[j], at(x, y, turn(z, d), core)).start()
        pltpu.make_async_copy(ints.at[:, :, cols], b_all.at[j, lo, z, :, :, half(hi)], b_one.at[j]).start()

    def two(j):
        await_bytes(b_all.at[j, 0, :, 0], b_one.at[j])
        for d in (1, 3):
            block = b_all.at[j, :, z, 0]
            send(block, block, b_send.at[j], b_two.at[j], at(x, y, turn(z, d), core)).start()
            block = b_all.at[j, lo, :, 1, :, half(hi)]
            send(block, block, b_send.at[j], b_two.at[j], at(turn(x, d), y, z, core)).start()

    def three(j):
        await_bytes(b_all.at[j, :, :, 0], b_two.at[j])
        for i, d in enumerate((1, 3)):
            block = b_all.at[j, i, turn(z, 4 - d), 0]
            send(block, block, b_send.at[j], b_three.at[j], at(x, y, turn(z, d), core)).start()
            source = turn(x, 4 - d)
            block = b_all.at[j, source % 2, pl.ds(2 * i, 2), 1, :, half(source // 2)]
            send(block, block, b_send.at[j], b_three.at[j], at(turn(x, d), y, z, core)).start()

    def deliver(j, y_to):
        for k in range(2):
            for h in range(2):
                src = o_all.at[j, y_to, pl.ds(k * 128, 128), pl.ds(h * W, W)]
                dst = out.at[:, pl.ds(pl.multiple_of((h * 8 + y * 2 + core) * (steps * W) + j * W, W), W)]
                own = jnp.logical_and(y_to == y, core == k)

                @pl.when(own)
                def _():
                    pltpu.make_async_copy(src, dst, o_recv.at[j]).start()

                @pl.when(jnp.logical_not(own))
                def _():
                    send(src, dst, o_send.at[j], o_recv.at[j], at(x, y_to, z, k)).start()

    def compute(j):
        await_bytes(b_all.at[j, 0, :, 0], b_three.at[j])

        def tile(m, _):
            y_to = turn(y, m + 2)
            block = jnp.dot(
                a_all[pl.ds(2 * y_to, 2)].reshape(256, 2048), b_all[j].reshape(16 * 128, 2 * W), preferred_element_type=jnp.float32
            )
            o_all[j, y_to] = block.astype(jnp.bfloat16)
            deliver(j, y_to)
            return 0

        lax.fori_loop(0, 4, tile, 0)

    mine = a_all.at[2 * y + core]

    def amplitudes_start():
        pltpu.make_async_copy(amps, mine, a_core).start()
        send(amps, mine, a_send, a_near, at(x, turn(y, 1), z, core)).start()
        send(amps, mine, a_send, a_near, at(x, turn(y, 3), z, core)).start()
        send(amps, mine, a_send, a_far, at(x, turn(y, 2), z, core)).start()
        send(amps, mine, a_send, a_core, at(x, y, z, 1 - core)).start()

    def to_core(y_of):
        block = a_all.at[2 * y_of + core]
        send(block, block, a_send, a_core, at(x, y, z, 1 - core)).start()

    def step(t, _):
        @pl.when(jnp.logical_and(t >= 2, t < steps + 2))
        def _():
            three(t - 2)

        @pl.when(jnp.logical_and(t >= 1, t < steps + 1))
        def _():
            two(t - 1)

        @pl.when(t < steps)
        def _():
            one(t)

        @pl.when(t == 0)
        def _():
            amplitudes_start()

        @pl.when(t == 2)
        def _():
            await_bytes(a_all.at[pl.ds(0, 2)], a_near)
            to_core(turn(y, 1))
            to_core(turn(y, 3))

        @pl.when(t == 3)
        def _():
            await_bytes(a_all.at[0], a_far)
            to_core(turn(y, 2))
            await_bytes(a_all.at[pl.ds(0, 5)], a_core)

        @pl.when(t >= 3)
        def _():
            compute(t - 3)

        return 0

    lax.fori_loop(0, steps + 3, step, 0)

    await_bytes(a_all.at[pl.ds(0, 7)], a_send)

    def drain(j, _):
        await_bytes(out.at[:, pl.ds(0, 30 * W)], b_send.at[j])
        await_bytes(out.at[pl.ds(0, 112), pl.ds(0, 16 * W)], o_send.at[j])
        await_bytes(out.at[:, pl.ds(0, 16 * W)], o_recv.at[j])
        return 0

    lax.fori_loop(0, steps, drain, 0)


def emit(src, dst, sem):
    rows = src.shape[0] // PARTS
    copies = [pltpu.make_async_copy(src.at[pl.ds(i * rows, rows)], dst.at[pl.ds(i * rows, rows)], sem.at[i]) for i in range(PARTS)]
    for copy in copies:
        copy.start()
    for copy in copies:
        copy.wait()


def body(amplitudes, integrals):
    depth, width = integrals.shape
    steps = width // W
    sem = pltpu.SemaphoreType.DMA
    held = pl.pallas_call(
        functools.partial(kernel, steps),
        out_shape=pltpu.VMEM((128, 16 * width), jnp.bfloat16),
        in_specs=[pl.BlockSpec(memory_space=pl.ANY)] * 2,
        out_specs=pl.BlockSpec(memory_space=pl.ANY),
        scratch_shapes=[
            pltpu.VMEM((8, 128, 2048), jnp.bfloat16),
            pltpu.VMEM((steps, 2, 4, 2, 128, 2 * W), jnp.bfloat16),
            pltpu.VMEM((steps, 4, 256, 2 * W), jnp.bfloat16),
            sem, sem, sem, sem,
            sem((steps,)), sem((steps,)), sem((steps,)), sem((steps,)), sem((steps,)), sem((steps,)),
        ],
        compiler_params=pltpu.CompilerParams(
            collective_id=0, has_side_effects=True, vmem_limit_bytes=54000000
        ),
    )(amplitudes, integrals.reshape(2, depth // 2, width))
    return pl.pallas_call(
        emit,
        out_shape=jax.ShapeDtypeStruct(held.shape, held.dtype),
        in_specs=[pl.BlockSpec(memory_space=pltpu.VMEM)],
        out_specs=pl.BlockSpec(memory_space=pl.ANY),
        scratch_shapes=[sem((PARTS,))],
        compiler_params=pltpu.CompilerParams(vmem_limit_bytes=1_000_000),
    )(held)


def solution(mesh):
    placed = (P(("row", "col"), None), P("row", "col"))
    return jax.shard_map(
        body, mesh=mesh, in_specs=placed, out_specs=P(("row", "col"), None), check_vma=False
    )
```

```python
import functools

import jax
import jax.numpy as jnp
from jax import lax
from jax.experimental import pallas as pl
from jax.experimental.pallas import tpu as pltpu
from jax.sharding import PartitionSpec as P

MESH = pl.DeviceIdType.MESH
PARTS = 8
HEAD, REST = (1, 256), (11, 256)


class Phase:
    def __init__(self, shape, first, start, refs):
        self.steps, self.w = shape
        self.first, self.start = first, start
        self.b, self.o, self.one, self.on, self.two, self.three, self.b_send, self.o_recv, self.o_send = refs

    def cols(self, j, base=0):
        return pl.ds(pl.multiple_of(base + self.start + j * self.w, 128), self.w)

    def block(self, h):
        return pl.ds(pl.multiple_of(h * self.w, self.w), self.w)


def kernel(amps, ints, out, a_all, a_near, a_far, a_own, a_core_near, a_core_far, a_send, *refs):
    row, col = lax.axis_index("row"), lax.axis_index("col")
    hi, lo, y, z, core = col // 8, row // 4, (col // 2) % 4, row % 4, col % 2
    x = hi * 2 + lo
    width = ints.shape[2]
    phases = [Phase(HEAD, 0, 0, refs[:9]), Phase(REST, HEAD[0], HEAD[0] * HEAD[1], refs[9:])]
    total = HEAD[0] + REST[0]

    def at(x, y, z, core):
        return ((x % 2) * 4 + z, (x // 2) * 8 + y * 2 + core)

    def turn(v, by):
        return (v + by) % 4

    def send(src, dst, send_sem, recv_sem, device):
        pltpu.make_async_remote_copy(
            src_ref=src, dst_ref=dst, send_sem=send_sem, recv_sem=recv_sem, device_id=device, device_id_type=MESH
        ).start()

    def await_bytes(ref, sem):
        pltpu.make_async_copy(ref, ref, sem).wait()

    barrier = pltpu.get_barrier_semaphore()
    ring = [1, 3, 2]
    partners = [at(turn(x, d), y, z, core) for d in (1, 3)] + [at(x, y, turn(z, d), core) for d in (1, 3)]
    partners += [at(x, turn(y, d), z, core) for d in ring] + [at(x, turn(y, d), z, 1 - core) for d in [0] + ring]
    for device in partners:
        pl.semaphore_signal(barrier, inc=1, device_id=device, device_id_type=MESH)
    pl.semaphore_wait(barrier, len(partners))

    def one(p, j):
        for d in (1, 3):
            send(ints.at[0, :, p.cols(j)], p.b.at[j, lo, z, 0, :, p.block(hi)], p.b_send.at[j], p.one.at[j], at(turn(x, d), y, z, core))
            send(ints.at[1, :, p.cols(j)], p.b.at[j, lo, z, 1, :, p.block(hi)], p.b_send.at[j], p.one.at[j], at(x, y, turn(z, d), core))
        pltpu.make_async_copy(ints.at[:, :, p.cols(j)], p.b.at[j, lo, z, :, :, p.block(hi)], p.one.at[j]).start()

    def on(p, j):
        await_bytes(p.b.at[j, 0, pl.ds(0, 3), 0], p.one.at[j])
        for i, d in enumerate((1, 3)):
            source = turn(x, 4 - d)
            block = p.b.at[j, source % 2, z, 0, pl.ds(64 * i, 64), p.block(source // 2)]
            send(block, block, p.b_send.at[j], p.on.at[j], at(turn(x, d), y, z, core))
            block = p.b.at[j, lo, turn(z, 4 - d), 1, pl.ds(64 * i, 64), p.block(hi)]
            send(block, block, p.b_send.at[j], p.on.at[j], at(x, y, turn(z, d), core))

    def two(p, j):
        await_bytes(p.b.at[j, 0, 0, 0], p.on.at[j])
        for d in (1, 3):
            block = p.b.at[j, :, z, 0]
            send(block, block, p.b_send.at[j], p.two.at[j], at(x, y, turn(z, d), core))
            block = p.b.at[j, lo, :, 1, :, p.block(hi)]
            send(block, block, p.b_send.at[j], p.two.at[j], at(turn(x, d), y, z, core))

    def three(p, j):
        await_bytes(p.b.at[j, :, :, 0], p.two.at[j])
        for i, d in enumerate((1, 3)):
            block = p.b.at[j, i, turn(z, 4 - d), 0]
            send(block, block, p.b_send.at[j], p.three.at[j], at(x, y, turn(z, d), core))
            source = turn(x, 4 - d)
            block = p.b.at[j, source % 2, pl.ds(2 * i, 2), 1, :, p.block(source // 2)]
            send(block, block, p.b_send.at[j], p.three.at[j], at(turn(x, d), y, z, core))

    def deliver(p, j, y_to):
        for k in range(2):
            for h in range(2):
                src = p.o.at[j, y_to, pl.ds(k * 128, 128), pl.ds(h * p.w, p.w)]
                dst = out.at[:, p.cols(j, (h * 8 + y * 2 + core) * width)]
                own = jnp.logical_and(y_to == y, core == k)

                @pl.when(own)
                def _():
                    pltpu.make_async_copy(src, dst, p.o_recv.at[j]).start()

                @pl.when(jnp.logical_not(own))
                def _():
                    send(src, dst, p.o_send.at[j], p.o_recv.at[j], at(x, y_to, z, k))

    def arrived(p, j):
        await_bytes(p.b.at[j, 0, :, 0], p.three.at[j])

    def compute(p, j):
        arrived(p, j)
        tiles(p, j, 0, 4)

    def tiles(p, j, first, last):
        def tile(m, _):
            y_to = turn(y, jnp.where(m == 0, 1, jnp.where(m == 1, 3, jnp.where(m == 2, 0, 2))))
            block = jnp.dot(
                a_all[pl.ds(2 * y_to, 2)].reshape(256, 2048),
                p.b[j].reshape(16 * 128, 2 * p.w),
                preferred_element_type=jnp.float32,
            )
            p.o[j, y_to] = block.astype(jnp.bfloat16)
            deliver(p, j, y_to)
            return 0

        lax.fori_loop(first, last, tile, 0)

    def to_core(y_of, sem):
        block = a_all.at[2 * y_of + core]
        send(block, block, a_send, sem, at(x, y, z, 1 - core))

    def amplitudes_start():
        mine = a_all.at[2 * y + core]
        send(amps, mine, a_send, a_near, at(x, turn(y, 1), z, core))
        send(amps, mine, a_send, a_near, at(x, turn(y, 3), z, core))
        send(amps, mine, a_send, a_own, at(x, y, z, 1 - core))
        pltpu.make_async_copy(amps, mine, a_own).start()

    def amplitudes_near():
        await_bytes(a_all.at[pl.ds(0, 2)], a_near)
        for i, d in enumerate((1, 3)):
            block = a_all.at[2 * turn(y, 4 - d) + core, pl.ds(64 * i, 64)]
            send(block, block, a_send, a_far, at(x, turn(y, d), z, core))
        to_core(turn(y, 1), a_core_near)
        to_core(turn(y, 3), a_core_near)
        await_bytes(a_all.at[pl.ds(0, 2)], a_own)
        await_bytes(a_all.at[pl.ds(0, 2)], a_core_near)

    def amplitudes_far():
        await_bytes(a_all.at[0], a_far)
        to_core(turn(y, 2), a_core_far)
        await_bytes(a_all.at[0], a_core_far)

    def stage(work, j):
        for p in phases:

            @pl.when(jnp.logical_and(j >= p.first, j < p.first + p.steps))
            def _():
                work(p, j - p.first)

    def step(t, _):
        @pl.when(t == 4)
        def _():
            amplitudes_near()
            arrived(phases[0], 0)
            tiles(phases[0], 0, 0, 3)

        stage(three, t - 3)
        stage(two, t - 2)
        stage(on, t - 1)
        stage(one, t)

        @pl.when(t == 0)
        def _():
            amplitudes_start()

        @pl.when(t == 4)
        def _():
            amplitudes_far()
            tiles(phases[0], 0, 3, 4)

        @pl.when(t > 4)
        def _():
            stage(compute, t - 4)

        return 0

    lax.fori_loop(0, total + 4, step, 0)

    await_bytes(a_all.at[pl.ds(0, 7)], a_send)

    for p in phases:

        def drain(j, _):
            await_bytes(out.at[:, pl.ds(0, 30 * p.w)], p.b_send.at[j])
            await_bytes(out.at[pl.ds(0, 112), pl.ds(0, 16 * p.w)], p.o_send.at[j])
            await_bytes(out.at[:, pl.ds(0, 16 * p.w)], p.o_recv.at[j])
            return 0

        lax.fori_loop(0, p.steps, drain, 0)


def emit(src, dst, sem):
    rows = src.shape[0] // PARTS
    copies = [pltpu.make_async_copy(src.at[pl.ds(i * rows, rows)], dst.at[pl.ds(i * rows, rows)], sem.at[i]) for i in range(PARTS)]
    for copy in copies:
        copy.start()
    for copy in copies:
        copy.wait()


def body(amplitudes, integrals):
    depth, width = integrals.shape
    sem = pltpu.SemaphoreType.DMA
    scratch = [pltpu.VMEM((8, 128, 2048), jnp.bfloat16)] + [sem] * 6
    for steps, w in (HEAD, REST):
        scratch += [
            pltpu.VMEM((steps, 2, 4, 2, 128, 2 * w), jnp.bfloat16),
            pltpu.VMEM((steps, 4, 256, 2 * w), jnp.bfloat16),
        ] + [sem((steps,))] * 7
    held = pl.pallas_call(
        kernel,
        out_shape=pltpu.VMEM((128, 16 * width), jnp.bfloat16),
        in_specs=[pl.BlockSpec(memory_space=pl.ANY)] * 2,
        out_specs=pl.BlockSpec(memory_space=pl.ANY),
        scratch_shapes=scratch,
        compiler_params=pltpu.CompilerParams(
            collective_id=0, has_side_effects=True, vmem_limit_bytes=54_000_000
        ),
    )(amplitudes, integrals.reshape(2, depth // 2, width))
    return pl.pallas_call(
        emit,
        out_shape=jax.ShapeDtypeStruct(held.shape, held.dtype),
        in_specs=[pl.BlockSpec(memory_space=pltpu.VMEM)],
        out_specs=pl.BlockSpec(memory_space=pl.ANY),
        scratch_shapes=[sem((PARTS,))],
        compiler_params=pltpu.CompilerParams(vmem_limit_bytes=1_000_000),
    )(held)


def solution(mesh):
    placed = (P(("row", "col"), None), P("row", "col"))
    return jax.shard_map(
        body, mesh=mesh, in_specs=placed, out_specs=P(("row", "col"), None), check_vma=False
    )
```

```python
import functools

import jax
import jax.numpy as jnp
from jax import lax
from jax.experimental import pallas as pl
from jax.experimental.pallas import tpu as pltpu
from jax.sharding import PartitionSpec as P

MESH = pl.DeviceIdType.MESH
PARTS = 8
HEAD, REST = (1, 128), (23, 128)


class Phase:
    def __init__(self, shape, first, start, refs):
        self.steps, self.w = shape
        self.first, self.start = first, start
        self.b, self.o, self.one, self.rest_one, self.on, self.two, self.rest_two, self.three, self.b_send, self.o_recv, self.o_send = refs

    def cols(self, j, base=0):
        return pl.ds(pl.multiple_of(base + self.start + j * self.w, 128), self.w)

    def block(self, h):
        return pl.ds(pl.multiple_of(h * self.w, self.w), self.w)


def kernel(amps, ints, out, a_all, a_first, a_second, a_far, a_own, a_core_near, a_core_far, a_send, *refs):
    row, col = lax.axis_index("row"), lax.axis_index("col")
    hi, lo, y, z, core = col // 8, row // 4, (col // 2) % 4, row % 4, col % 2
    x = hi * 2 + lo
    width = ints.shape[2]
    phases = [Phase(HEAD, 0, 0, refs[:11]), Phase(REST, HEAD[0], HEAD[0] * HEAD[1], refs[11:])]
    total = HEAD[0] + REST[0]

    def at(x, y, z, core):
        return ((x % 2) * 4 + z, (x // 2) * 8 + y * 2 + core)

    def turn(v, by):
        return (v + by) % 4

    def send(src, dst, send_sem, recv_sem, device):
        pltpu.make_async_remote_copy(
            src_ref=src, dst_ref=dst, send_sem=send_sem, recv_sem=recv_sem, device_id=device, device_id_type=MESH
        ).start()

    def await_bytes(ref, sem):
        pltpu.make_async_copy(ref, ref, sem).wait()

    barrier = pltpu.get_barrier_semaphore()
    ring = [1, 3, 2]
    partners = [at(turn(x, d), y, z, core) for d in (1, 3)] + [at(x, y, turn(z, d), core) for d in (1, 3)]
    partners += [at(x, turn(y, d), z, core) for d in ring] + [at(x, turn(y, d), z, 1 - core) for d in [0] + ring]
    for device in partners:
        pl.semaphore_signal(barrier, inc=1, device_id=device, device_id_type=MESH)
    pl.semaphore_wait(barrier, len(partners))

    def one(p, j):
        for sem, flip in ((p.one, 0), (p.rest_one, 1)):
            for i, d in enumerate((1, 3)):
                rows = pl.ds(64 * (i ^ flip), 64)
                send(ints.at[0, rows, p.cols(j)], p.b.at[j, lo, z, 0, rows, p.block(hi)], p.b_send.at[j], sem.at[j], at(turn(x, d), y, z, core))
                send(ints.at[1, rows, p.cols(j)], p.b.at[j, lo, z, 1, rows, p.block(hi)], p.b_send.at[j], sem.at[j], at(x, y, turn(z, d), core))
        pltpu.make_async_copy(ints.at[:, :, p.cols(j)], p.b.at[j, lo, z, :, :, p.block(hi)], p.rest_one.at[j]).start()

    def on(p, j):
        await_bytes(p.b.at[j, 0, 0, 0], p.one.at[j])
        for i, d in enumerate((1, 3)):
            source = turn(x, 4 - d)
            block = p.b.at[j, source % 2, z, 0, pl.ds(64 * i, 64), p.block(source // 2)]
            send(block, block, p.b_send.at[j], p.on.at[j], at(turn(x, d), y, z, core))
            block = p.b.at[j, lo, turn(z, 4 - d), 1, pl.ds(64 * i, 64), p.block(hi)]
            send(block, block, p.b_send.at[j], p.on.at[j], at(x, y, turn(z, d), core))

    def two(p, j):
        await_bytes(p.b.at[j, 0, pl.ds(0, 2), 0], p.rest_one.at[j])
        await_bytes(p.b.at[j, 0, 0, 0], p.on.at[j])
        for sem, flip in ((p.two, 0), (p.rest_two, 1)):
            for i, d in enumerate((1, 3)):
                block = p.b.at[j, i ^ flip, z, 0]
                send(block, block, p.b_send.at[j], sem.at[j], at(x, y, turn(z, d), core))
                block = p.b.at[j, lo, pl.ds(2 * (i ^ flip), 2), 1, :, p.block(hi)]
                send(block, block, p.b_send.at[j], sem.at[j], at(turn(x, d), y, z, core))

    def three(p, j):
        await_bytes(p.b.at[j, 0, :, 0], p.two.at[j])
        for i, d in enumerate((1, 3)):
            block = p.b.at[j, i, turn(z, 4 - d), 0]
            send(block, block, p.b_send.at[j], p.three.at[j], at(x, y, turn(z, d), core))
            source = turn(x, 4 - d)
            block = p.b.at[j, source % 2, pl.ds(2 * i, 2), 1, :, p.block(source // 2)]
            send(block, block, p.b_send.at[j], p.three.at[j], at(turn(x, d), y, z, core))

    def deliver(p, j, y_to):
        for k in range(2):
            for h in range(2):
                src = p.o.at[j, y_to, pl.ds(k * 128, 128), pl.ds(h * p.w, p.w)]
                dst = out.at[:, p.cols(j, (h * 8 + y * 2 + core) * width)]
                own = jnp.logical_and(y_to == y, core == k)

                @pl.when(own)
                def _():
                    pltpu.make_async_copy(src, dst, p.o_recv.at[j]).start()

                @pl.when(jnp.logical_not(own))
                def _():
                    send(src, dst, p.o_send.at[j], p.o_recv.at[j], at(x, y_to, z, k))

    def arrived(p, j):
        await_bytes(p.b.at[j, 0, :, 0], p.rest_two.at[j])
        await_bytes(p.b.at[j, 0, :, 0], p.three.at[j])

    def compute(p, j):
        arrived(p, j)
        tiles(p, j, 0, 4)

    def tiles(p, j, first, last):
        def tile(m, _):
            y_to = turn(y, jnp.where(m == 0, 1, jnp.where(m == 1, 3, jnp.where(m == 2, 0, 2))))
            block = jnp.dot(
                a_all[pl.ds(2 * y_to, 2)].reshape(256, 2048),
                p.b[j].reshape(16 * 128, 2 * p.w),
                preferred_element_type=jnp.float32,
            )
            p.o[j, y_to] = block.astype(jnp.bfloat16)
            deliver(p, j, y_to)
            return 0

        lax.fori_loop(first, last, tile, 0)

    def to_core(y_of, sem):
        block = a_all.at[2 * y_of + core]
        send(block, block, a_send, sem, at(x, y, z, 1 - core))

    def amplitudes_start():
        mine = a_all.at[2 * y + core]
        for sem, flip in ((a_first, 0), (a_second, 1)):
            for i, d in enumerate((1, 3)):
                rows = pl.ds(64 * (i ^ flip), 64)
                send(amps.at[rows], mine.at[rows], a_send, sem, at(x, turn(y, d), z, core))
        send(amps, mine, a_send, a_own, at(x, y, z, 1 - core))
        pltpu.make_async_copy(amps, mine, a_own).start()

    def amplitudes_on():
        await_bytes(a_all.at[0], a_first)
        for i, d in enumerate((1, 3)):
            block = a_all.at[2 * turn(y, 4 - d) + core, pl.ds(64 * i, 64)]
            send(block, block, a_send, a_far, at(x, turn(y, d), z, core))

    def amplitudes_near():
        await_bytes(a_all.at[0], a_second)
        to_core(turn(y, 1), a_core_near)
        to_core(turn(y, 3), a_core_near)

    def amplitudes_ready():
        await_bytes(a_all.at[pl.ds(0, 2)], a_own)
        await_bytes(a_all.at[pl.ds(0, 2)], a_core_near)

    def amplitudes_far():
        await_bytes(a_all.at[0], a_far)
        to_core(turn(y, 2), a_core_far)
        await_bytes(a_all.at[0], a_core_far)

    def stage(work, j):
        for p in phases:

            @pl.when(jnp.logical_and(j >= p.first, j < p.first + p.steps))
            def _():
                work(p, j - p.first)

    def step(t, _):
        @pl.when(t == 4)
        def _():
            amplitudes_ready()
            arrived(phases[0], 0)
            tiles(phases[0], 0, 0, 3)

        stage(three, t - 3)
        stage(two, t - 2)
        stage(on, t - 1)
        stage(one, t)

        @pl.when(t == 0)
        def _():
            amplitudes_start()

        @pl.when(t == 2)
        def _():
            amplitudes_on()

        @pl.when(t == 3)
        def _():
            amplitudes_near()

        @pl.when(t == 4)
        def _():
            amplitudes_far()
            tiles(phases[0], 0, 3, 4)

        @pl.when(t > 4)
        def _():
            stage(compute, t - 4)

        return 0

    lax.fori_loop(0, total + 4, step, 0)

    await_bytes(a_all.at[pl.ds(0, 7)], a_send)

    for p in phases:

        def drain(j, _):
            await_bytes(out.at[:, pl.ds(0, 30 * p.w)], p.b_send.at[j])
            await_bytes(out.at[pl.ds(0, 112), pl.ds(0, 16 * p.w)], p.o_send.at[j])
            await_bytes(out.at[:, pl.ds(0, 16 * p.w)], p.o_recv.at[j])
            return 0

        lax.fori_loop(0, p.steps, drain, 0)


def emit(src, dst, sem):
    rows = src.shape[0] // PARTS
    copies = [pltpu.make_async_copy(src.at[pl.ds(i * rows, rows)], dst.at[pl.ds(i * rows, rows)], sem.at[i]) for i in range(PARTS)]
    for copy in copies:
        copy.start()
    for copy in copies:
        copy.wait()


def body(amplitudes, integrals):
    depth, width = integrals.shape
    sem = pltpu.SemaphoreType.DMA
    scratch = [pltpu.VMEM((8, 128, 2048), jnp.bfloat16)] + [sem] * 7
    for steps, w in (HEAD, REST):
        scratch += [
            pltpu.VMEM((steps, 2, 4, 2, 128, 2 * w), jnp.bfloat16),
            pltpu.VMEM((steps, 4, 256, 2 * w), jnp.bfloat16),
        ] + [sem((steps,))] * 9
    held = pl.pallas_call(
        kernel,
        out_shape=pltpu.VMEM((128, 16 * width), jnp.bfloat16),
        in_specs=[pl.BlockSpec(memory_space=pl.ANY)] * 2,
        out_specs=pl.BlockSpec(memory_space=pl.ANY),
        scratch_shapes=scratch,
        compiler_params=pltpu.CompilerParams(
            collective_id=0, has_side_effects=True, vmem_limit_bytes=54_000_000
        ),
    )(amplitudes, integrals.reshape(2, depth // 2, width))
    return pl.pallas_call(
        emit,
        out_shape=jax.ShapeDtypeStruct(held.shape, held.dtype),
        in_specs=[pl.BlockSpec(memory_space=pltpu.VMEM)],
        out_specs=pl.BlockSpec(memory_space=pl.ANY),
        scratch_shapes=[sem((PARTS,))],
        compiler_params=pltpu.CompilerParams(vmem_limit_bytes=1_000_000),
    )(held)


def solution(mesh):
    placed = (P(("row", "col"), None), P("row", "col"))
    return jax.shard_map(
        body, mesh=mesh, in_specs=placed, out_specs=P(("row", "col"), None), check_vma=False
    )
```

```python
import jax
import jax.numpy as jnp
from jax import lax
from jax.experimental import pallas as pl
from jax.experimental.pallas import tpu as pltpu
from jax.sharding import PartitionSpec as P

MESH = pl.DeviceIdType.MESH
GROUP, LAG = 4, 16
HEAD, REST = (1, 128), (23, 128)


class Phase:
    def __init__(self, shape, first, start, refs):
        self.steps, self.w = shape
        self.first, self.start = first, start
        self.b, self.o, self.one, self.rest_one, self.on, self.two, self.rest_two, self.three, self.b_send, self.o_recv, self.o_send = refs

    def cols(self, j, base=0):
        return pl.ds(pl.multiple_of(base + self.start + j * self.w, 128), self.w)

    def block(self, h):
        return pl.ds(pl.multiple_of(h * self.w, self.w), self.w)


def kernel(amps, ints, out, held, written, a_all, a_first, a_second, a_far, a_own, a_core_near, a_core_far, a_send, *refs):
    row, col = lax.axis_index("row"), lax.axis_index("col")
    hi, lo, y, z, core = col // 8, row // 4, (col // 2) % 4, row % 4, col % 2
    x = hi * 2 + lo
    width = ints.shape[2]
    phases = [Phase(HEAD, 0, 0, refs[:11]), Phase(REST, HEAD[0], HEAD[0] * HEAD[1], refs[11:])]
    total = HEAD[0] + REST[0]

    def at(x, y, z, core):
        return ((x % 2) * 4 + z, (x // 2) * 8 + y * 2 + core)

    def turn(v, by):
        return (v + by) % 4

    def send(src, dst, send_sem, recv_sem, device):
        pltpu.make_async_remote_copy(
            src_ref=src, dst_ref=dst, send_sem=send_sem, recv_sem=recv_sem, device_id=device, device_id_type=MESH
        ).start()

    def await_bytes(ref, sem):
        pltpu.make_async_copy(ref, ref, sem).wait()

    barrier = pltpu.get_barrier_semaphore()
    ring = [1, 3, 2]
    partners = [at(turn(x, d), y, z, core) for d in (1, 3)] + [at(x, y, turn(z, d), core) for d in (1, 3)]
    partners += [at(x, turn(y, d), z, core) for d in ring] + [at(x, turn(y, d), z, 1 - core) for d in [0] + ring]
    for device in partners:
        pl.semaphore_signal(barrier, inc=1, device_id=device, device_id_type=MESH)
    pl.semaphore_wait(barrier, len(partners))

    def one(p, j):
        for sem, flip in ((p.one, 0), (p.rest_one, 1)):
            for i, d in enumerate((1, 3)):
                rows = pl.ds(64 * (i ^ flip), 64)
                send(ints.at[0, rows, p.cols(j)], p.b.at[j, lo, z, 0, rows, p.block(hi)], p.b_send.at[j], sem.at[j], at(turn(x, d), y, z, core))
                send(ints.at[1, rows, p.cols(j)], p.b.at[j, lo, z, 1, rows, p.block(hi)], p.b_send.at[j], sem.at[j], at(x, y, turn(z, d), core))
        pltpu.make_async_copy(ints.at[:, :, p.cols(j)], p.b.at[j, lo, z, :, :, p.block(hi)], p.rest_one.at[j]).start()

    def on(p, j):
        await_bytes(p.b.at[j, 0, 0, 0], p.one.at[j])
        for i, d in enumerate((1, 3)):
            source = turn(x, 4 - d)
            block = p.b.at[j, source % 2, z, 0, pl.ds(64 * i, 64), p.block(source // 2)]
            send(block, block, p.b_send.at[j], p.on.at[j], at(turn(x, d), y, z, core))
            block = p.b.at[j, lo, turn(z, 4 - d), 1, pl.ds(64 * i, 64), p.block(hi)]
            send(block, block, p.b_send.at[j], p.on.at[j], at(x, y, turn(z, d), core))

    def two(p, j):
        await_bytes(p.b.at[j, 0, pl.ds(0, 2), 0], p.rest_one.at[j])
        await_bytes(p.b.at[j, 0, 0, 0], p.on.at[j])
        for sem, flip in ((p.two, 0), (p.rest_two, 1)):
            for i, d in enumerate((1, 3)):
                block = p.b.at[j, i ^ flip, z, 0]
                send(block, block, p.b_send.at[j], sem.at[j], at(x, y, turn(z, d), core))
                block = p.b.at[j, lo, pl.ds(2 * (i ^ flip), 2), 1, :, p.block(hi)]
                send(block, block, p.b_send.at[j], sem.at[j], at(turn(x, d), y, z, core))

    def three(p, j):
        await_bytes(p.b.at[j, 0, :, 0], p.two.at[j])
        for i, d in enumerate((1, 3)):
            block = p.b.at[j, i, turn(z, 4 - d), 0]
            send(block, block, p.b_send.at[j], p.three.at[j], at(x, y, turn(z, d), core))
            source = turn(x, 4 - d)
            block = p.b.at[j, source % 2, pl.ds(2 * i, 2), 1, :, p.block(source // 2)]
            send(block, block, p.b_send.at[j], p.three.at[j], at(turn(x, d), y, z, core))

    def deliver(p, j, y_to):
        for k in range(2):
            for h in range(2):
                src = p.o.at[j, y_to, pl.ds(k * 128, 128), pl.ds(h * p.w, p.w)]
                dst = held.at[:, p.cols(j, (h * 8 + y * 2 + core) * width)]
                own = jnp.logical_and(y_to == y, core == k)

                @pl.when(own)
                def _():
                    pltpu.make_async_copy(src, dst, p.o_recv.at[j]).start()

                @pl.when(jnp.logical_not(own))
                def _():
                    send(src, dst, p.o_send.at[j], p.o_recv.at[j], at(x, y_to, z, k))

    def arrived(p, j):
        await_bytes(p.b.at[j, 0, :, 0], p.rest_two.at[j])
        await_bytes(p.b.at[j, 0, :, 0], p.three.at[j])

    def compute(p, j):
        arrived(p, j)
        tiles(p, j, 0, 4)

    def tiles(p, j, first, last):
        def tile(m, _):
            y_to = turn(y, jnp.where(m == 0, 1, jnp.where(m == 1, 3, jnp.where(m == 2, 0, 2))))
            block = jnp.dot(
                a_all[pl.ds(2 * y_to, 2)].reshape(256, 2048),
                p.b[j].reshape(16 * 128, 2 * p.w),
                preferred_element_type=jnp.float32,
            )
            p.o[j, y_to] = block.astype(jnp.bfloat16)
            deliver(p, j, y_to)
            return 0

        lax.fori_loop(first, last, tile, 0)

    def to_core(y_of, sem):
        block = a_all.at[2 * y_of + core]
        send(block, block, a_send, sem, at(x, y, z, 1 - core))

    def amplitudes_start():
        mine = a_all.at[2 * y + core]
        for sem, flip in ((a_first, 0), (a_second, 1)):
            for i, d in enumerate((1, 3)):
                rows = pl.ds(64 * (i ^ flip), 64)
                send(amps.at[rows], mine.at[rows], a_send, sem, at(x, turn(y, d), z, core))
        send(amps, mine, a_send, a_own, at(x, y, z, 1 - core))
        pltpu.make_async_copy(amps, mine, a_own).start()

    def amplitudes_on():
        await_bytes(a_all.at[0], a_first)
        for i, d in enumerate((1, 3)):
            block = a_all.at[2 * turn(y, 4 - d) + core, pl.ds(64 * i, 64)]
            send(block, block, a_send, a_far, at(x, turn(y, d), z, core))

    def amplitudes_near():
        await_bytes(a_all.at[0], a_second)
        to_core(turn(y, 1), a_core_near)
        to_core(turn(y, 3), a_core_near)

    def amplitudes_ready():
        await_bytes(a_all.at[pl.ds(0, 2)], a_own)
        await_bytes(a_all.at[pl.ds(0, 2)], a_core_near)

    def amplitudes_far():
        await_bytes(a_all.at[0], a_far)
        to_core(turn(y, 2), a_core_far)
        await_bytes(a_all.at[0], a_core_far)

    def stage(work, j):
        for p in phases:

            @pl.when(jnp.logical_and(j >= p.first, j < p.first + p.steps))
            def _():
                work(p, j - p.first)

    def landed(p, j):
        await_bytes(held.at[:, pl.ds(0, 16 * p.w)], p.o_recv.at[j])

    def write(first, steps):
        for i in range(steps):
            stage(landed, first + i)
        for c in range(16):
            cols = pl.ds(pl.multiple_of(c * width + first * 128, 128), steps * 128)
            pltpu.make_async_copy(held.at[:, cols], out.at[:, cols], written).start()

    def step(t, _):
        @pl.when(t == 4)
        def _():
            amplitudes_ready()
            arrived(phases[0], 0)
            tiles(phases[0], 0, 0, 3)

        stage(three, t - 3)
        stage(two, t - 2)
        stage(on, t - 1)
        stage(one, t)

        @pl.when(t == 0)
        def _():
            amplitudes_start()

        @pl.when(t == 2)
        def _():
            amplitudes_on()

        @pl.when(t == 3)
        def _():
            amplitudes_near()

        @pl.when(t == 4)
        def _():
            amplitudes_far()
            tiles(phases[0], 0, 3, 4)

        @pl.when(t > 4)
        def _():
            stage(compute, t - 4)

        @pl.when(jnp.logical_and(t >= LAG, t % GROUP == 0))
        def _():
            write(t - LAG, GROUP)

        return 0

    lax.fori_loop(0, total + 4, step, 0)
    late = range(LAG, total + 4, GROUP)[-1] - LAG + GROUP
    for first in range(late, total - GROUP, GROUP):
        write(first, GROUP)
    for first in range(total - GROUP, total):
        write(first, 1)

    await_bytes(a_all.at[pl.ds(0, 7)], a_send)

    for p in phases:

        def drain(j, _):
            await_bytes(held.at[:, pl.ds(0, 30 * p.w)], p.b_send.at[j])
            await_bytes(held.at[pl.ds(0, 112), pl.ds(0, 16 * p.w)], p.o_send.at[j])
            return 0

        lax.fori_loop(0, p.steps, drain, 0)

    await_bytes(held, written)


def body(amplitudes, integrals):
    depth, width = integrals.shape
    sem = pltpu.SemaphoreType.DMA
    scratch = [pltpu.VMEM((128, 16 * width), jnp.bfloat16), sem, pltpu.VMEM((8, 128, 2048), jnp.bfloat16)] + [sem] * 7
    for steps, w in (HEAD, REST):
        scratch += [
            pltpu.VMEM((steps, 2, 4, 2, 128, 2 * w), jnp.bfloat16),
            pltpu.VMEM((steps, 4, 256, 2 * w), jnp.bfloat16),
        ] + [sem((steps,))] * 9
    return pl.pallas_call(
        kernel,
        out_shape=jax.ShapeDtypeStruct((128, 16 * width), jnp.bfloat16),
        in_specs=[pl.BlockSpec(memory_space=pl.ANY)] * 2,
        out_specs=pl.BlockSpec(memory_space=pltpu.HBM),
        scratch_shapes=scratch,
        compiler_params=pltpu.CompilerParams(
            collective_id=0, has_side_effects=True, vmem_limit_bytes=60_000_000
        ),
    )(amplitudes, integrals.reshape(2, depth // 2, width))


def solution(mesh):
    placed = (P(("row", "col"), None), P("row", "col"))
    return jax.shard_map(
        body, mesh=mesh, in_specs=placed, out_specs=P(("row", "col"), None), check_vma=False
    )
```
